256 devices in a mesh: shot: 32 (over z, x_hi, core), dom: 8 (over y, x_lo).
Axes of the slice: x: 4 (x_hi: 2, x_lo: 2; x = x_hi * 2 + x_lo), y: 4, z: 8, core: 2. Of those that a mesh axis runs over, the one named last changes fastest.
Arguments:
- velocity: float32 [64, 128, 256], P('dom', 'shot'), may hold values from 0.15 to 0.4
- epsilon: float32 [64, 128, 256], P('dom', 'shot'), may hold values from 0.05 to 0.3
- forward_state: float32 [32, 4, 64, 128, 256], P('shot', None, 'dom'), may hold values from -1.2 to 1.2
- adjoint_state: float32 [32, 4, 64, 128, 256], P('shot', None, 'dom'), may hold values from -1.2 to 1.2
- source_cell: int32 [32], P('shot'), may hold values from 0 to 2097151
- wavelet: float32 [32, 3], P('shot'), may hold values from -6 to 6
- receiver_cells: int32 [32, 256], P('shot'), may hold values from 0 to 2097151
- residuals: float32 [32, 4, 256], P('shot'), may hold values from -6 to 6
Outputs:
- velocity_grad: float32 [64, 128, 256], P('dom', 'shot')
- epsilon_grad: float32 [64, 128, 256], P('dom', 'shot')
The draws below stay inside these ranges and needn't reach their ends.
Inputs may be any that keep to these rules, and one draw needn't show every extreme that they name: `source_cell`: flat grid cell index (z * 128 + x) * 256 + y of each shot's source. `receiver_cells`: flat grid cell indices (z * 128 + x) * 256 + y of each shot's receivers; two receivers may share a cell.
All inputs are finite; a program needn't handle non-finite values.
Results may differ from the reference program's by a relative error of at most 0.00002.
Values sent between devices are 32-bit elements; how exact they have to be, the bound alone decides.
No kernel may reach another device: no remote copies, remote signals or barrier semaphores. Data moves between devices by JAX's collectives and lax.ppermute only.
A program may use at most 128 MiB of HBM per device.

```python
import math
import jax
import jax.numpy as jnp
from jax import lax

NX = 128
NY = 256
NREC = 256
STEPS = 4
SHOTS = 32
NZ = 64


def place_ends(drawn, rng, smallest, largest):
    shape = drawn.shape
    place = [jax.random.randint(jax.random.fold_in(rng, axis), (), 0, shape[axis]) for axis in range(len(shape))]
    drawn = drawn.at[tuple(place)].set(smallest)
    longest = shape.index(max(shape))
    place[longest] = (place[longest] + 1) % shape[longest]
    return drawn.at[tuple(place)].set(largest)


def level_of(rng, extent, pieces, least, largest):
    level = 1.0
    for dim, parts in pieces:
        heights = jax.random.uniform(jax.random.fold_in(jax.random.fold_in(rng, 6), dim), (parts,), jnp.float32, least / len(pieces), largest / len(pieces))
        level = level * jnp.repeat(jnp.exp(heights), extent[dim] // parts).reshape((-1,) + (1,) * (len(extent) - 1 - dim))
    return level


def centred(key, shape, spread, limit, pieces=(), dtype=jnp.bfloat16):
    result = jax.random.normal(key, shape, jnp.float32) * spread
    if len(pieces) > 0:
        result = level_of(key, shape, pieces, -0.22, 0.18) * result
    return jnp.clip(result, min=-limit, max=limit).astype(dtype)


def setup_inputs(seed: int = 0) -> dict:
    splits = jax.random.split(jax.random.key(seed), 9)
    return {
        "velocity": jnp.clip(jnp.exp(math.log(0.4) - 0.98082923 * jax.random.uniform(splits[0], (NZ, NX, NY), jnp.float32) ** level_of(splits[0], (NZ, NX, NY), ((0, 8), (1, 32)), -0.2, 0.2)), 0.15, 0.4),
        "epsilon": jnp.clip(jnp.exp(math.log(0.3) - 1.7917595 * jax.random.uniform(splits[1], (NZ, NX, NY), jnp.float32) ** level_of(splits[1], (NZ, NX, NY), ((0, 8), (1, 32)), -0.2, 0.2)), 0.05, 0.3),
        "forward_state": centred(splits[2], (SHOTS, 4, NZ, NX, NY), 0.2, 1.2, ((0, 32), (2, 8)), jnp.float32),
        "adjoint_state": centred(splits[3], (SHOTS, 4, NZ, NX, NY), 0.2, 1.2, ((0, 32), (2, 8)), jnp.float32),
        "source_cell": place_ends(jax.random.randint(splits[4], (SHOTS,), 0, NZ * NX * NY), jax.random.fold_in(splits[4], 1), 0, (NZ * NX * NY) - 1).astype(jnp.int32),
        "wavelet": centred(splits[5], (SHOTS, STEPS - 1), 1.0, 6.0, ((0, 32),), jnp.float32),
        "receiver_cells": place_ends(jax.random.randint(splits[6], (SHOTS, NREC), 0, NZ * NX * NY), jax.random.fold_in(splits[6], 1), 0, (NZ * NX * NY) - 1).astype(jnp.int32),
        "residuals": centred(splits[7], (SHOTS, STEPS, NREC), 1.0, 6.0, ((0, 32),), jnp.float32),
    }


def stencil(padded, axis, size):
    def part(offset):
        return lax.slice_in_dim(padded, offset, offset + size, axis=axis)
    return (4.0 / 3.0) * (part(1) + part(3)) - (1.0 / 12.0) * (part(0) + part(4)) - 2.5 * part(2)


def second_diff(field, axis):
    widths = [(0, 0), (0, 0), (0, 0)]
    widths[axis] = (2, 2)
    return stencil(jnp.pad(field, widths), axis, field.shape[axis])


def lateral(field):
    return second_diff(field, 1) + second_diff(field, 2)


def inject(field, cell_ids, amounts):
    return field.reshape(-1).at[cell_ids].add(amounts).reshape(field.shape)


def reference(velocity, epsilon, forward_state, adjoint_state, source_cell, wavelet, receiver_cells, residuals):
    stiffness = velocity * velocity
    stretch = 1.0 + 2.0 * epsilon

    def one_shot(carry, item):
        fstate, astate, source, pulses, receivers, traces = item
        pressure_old, pressure_now, support_old, support_now = fstate[0], fstate[1], fstate[2], fstate[3]
        flat_terms = []
        depth_terms = []
        for moment in range(STEPS):
            flat_term = lateral(pressure_now)
            depth_term = second_diff(support_now, 0)
            flat_terms.append(flat_term)
            depth_terms.append(depth_term)
            if moment + 1 < STEPS:
                pressure_new = 2.0 * pressure_now - pressure_old + stiffness * (stretch * flat_term + depth_term)
                support_new = 2.0 * support_now - support_old + stiffness * (flat_term + depth_term)
                pressure_new = inject(pressure_new, source, pulses[moment])
                support_new = inject(support_new, source, pulses[moment])
                pressure_old, pressure_now = pressure_now, pressure_new
                support_old, support_now = support_now, support_new
        back_old, back_now, side_old, side_now = astate[0], astate[1], astate[2], astate[3]
        image_one = jnp.zeros_like(velocity)
        image_two = jnp.zeros_like(velocity)
        for moment in reversed(range(STEPS)):
            back_new = 2.0 * back_now - back_old + lateral(stiffness * (stretch * back_now + side_now))
            back_new = inject(back_new, receivers, traces[moment])
            side_new = 2.0 * side_now - side_old + second_diff(stiffness * (back_now + side_now), 0)
            image_one = image_one + back_new * flat_terms[moment]
            image_two = image_two + back_new * depth_terms[moment] + side_new * (flat_terms[moment] + depth_terms[moment])
            back_old, back_now = back_now, back_new
            side_old, side_now = side_now, side_new
        return (carry[0] + image_one, carry[1] + image_two), None

    start = (jnp.zeros_like(velocity), jnp.zeros_like(velocity))
    totals, unused = lax.scan(one_shot, start, (forward_state, adjoint_state, source_cell, wavelet, receiver_cells, residuals))
    velocity_grad = 2.0 * velocity * (stretch * totals[0] + totals[1])
    epsilon_grad = 2.0 * stiffness * totals[0]
    return velocity_grad, epsilon_grad
```

```python
import functools

import jax
import jax.numpy as jnp
from jax import lax
from jax.experimental import pallas as pl
from jax.experimental.pallas import tpu as pltpu
from jax.sharding import PartitionSpec as P

STEPS = 4
ROWS = 32
UP, DOWN = 4.0 / 3.0, 1.0 / 12.0
VMEM = pl.BlockSpec(memory_space=pltpu.VMEM)
SMEM = pl.BlockSpec(memory_space=pltpu.SMEM)


def shape(*dims):
    return jax.ShapeDtypeStruct(dims, jnp.float32)


def call(body, outs, args, scalars=0, scratch=(), out_specs=None, work=1.0):
    specs = [SMEM] * scalars + [VMEM] * (len(args) - scalars)
    size = sum(4 * a.size for a in args) + sum(4 * o.size for o in outs)
    return pl.pallas_call(
        body,
        out_shape=tuple(outs),
        in_specs=specs,
        out_specs=tuple(out_specs or [VMEM] * len(outs)),
        scratch_shapes=list(scratch),
        compiler_params=pltpu.CompilerParams(vmem_limit_bytes=48 * 1024 * 1024),
        cost_estimate=pl.CostEstimate(
            flops=int(work * size * 4), bytes_accessed=size, transcendentals=0
        ),
    )(*args)


def edge_rows(load, start, count):
    parts = []
    low, high = max(start - 8, 0), min(start + ROWS + 8, count)
    body = load(low, high - low)
    blank = jnp.zeros((8, body.shape[1]), jnp.float32)
    if start == 0:
        parts.append(blank)
    parts.append(body)
    if start + ROWS == count:
        parts.append(blank)
    return jnp.concatenate(parts, axis=0) if len(parts) > 1 else body


def lateral(wide, lanes):
    rows, length = wide.shape
    mid = wide[8 : 8 + ROWS]

    def x_at(shift):
        return pltpu.roll(wide, shift % rows, 0)[8 : 8 + ROWS]

    def y_at(shift):
        moved = pltpu.roll(mid, shift % length, 1)
        keep = lanes >= shift if shift > 0 else lanes < length + shift
        return jnp.where(keep, moved, 0.0)

    near = (x_at(1) + x_at(-1)) + (y_at(1) + y_at(-1))
    far = (x_at(2) + x_at(-2)) + (y_at(2) + y_at(-2))
    return UP * near - DOWN * far - 5.0 * mid


def vertical(ext, layer, rows):
    def at(offset):
        return ext[layer + offset, rows, :]

    return UP * (at(1) + at(3)) - DOWN * (at(0) + at(4)) - 2.5 * at(2)


def fill(ext, lo, hi):
    depth = ext.shape[0] - 4
    ext[0:2] = lo[...]
    ext[depth + 2 : depth + 4] = hi[...]


def put_ends(ref, ext_or_val, lo_out, hi_out):
    depth = ref.shape[0]
    lo_out[...] = ref[0:2]
    hi_out[...] = ref[depth - 2 : depth]


def forward_kernel(moment, with_image, last, *refs):
    it = iter(refs)
    info, pulse = next(it), next(it)
    p_now, q_now, lo, hi = next(it), next(it), next(it), next(it)
    if not last:
        p_old, q_old, stiff, stretch = next(it), next(it), next(it), next(it)
    if with_image:
        back, side = next(it), next(it)
    if with_image and last:
        one_in, two_in = next(it), next(it)
    if not last:
        p_out, q_out, lo_out, hi_out = next(it), next(it), next(it), next(it)
    first_out, second_out = next(it), next(it)
    ext = next(it)
    depth, width, length = p_now.shape
    fill(ext, lo, hi)
    lanes = lax.broadcasted_iota(jnp.int32, (ROWS, length), 1)
    place = lax.broadcasted_iota(jnp.int32, (ROWS, length), 0) * length + lanes

    def copy(layer, _):
        ext[layer + 2] = q_now[layer]
        return 0

    lax.fori_loop(0, depth, copy, 0)
    here = info[1] - info[0]
    amount = pulse[0, moment] if not last else 0.0

    def step(layer, _):
        for start in range(0, width, ROWS):
            rows = pl.ds(start, ROWS)
            flat = lateral(edge_rows(lambda s, n: p_now[layer, pl.ds(s, n), :], start, width), lanes)
            deep = vertical(ext, layer, rows)
            if not last:
                k = stiff[layer, rows, :]
                hit = place == here - (layer * width + start) * length
                add = jnp.where(hit, amount, 0.0)
                p = (
                    2.0 * p_now[layer, rows, :]
                    - p_old[layer, rows, :]
                    + k * (stretch[layer, rows, :] * flat + deep)
                )
                q = 2.0 * q_now[layer, rows, :] - q_old[layer, rows, :] + k * (flat + deep)
                p_out[layer, rows, :] = p + add
                q_out[layer, rows, :] = q + add
            if with_image:
                a, b = back[layer, rows, :], side[layer, rows, :]
                one = a * flat
                two = a * deep + b * (flat + deep)
                if last:
                    one = one + one_in[layer, rows, :]
                    two = two + two_in[layer, rows, :]
                first_out[layer, rows, :] = one
                second_out[layer, rows, :] = two
            else:
                first_out[layer, rows, :] = flat
                second_out[layer, rows, :] = deep
        return 0

    lax.fori_loop(0, depth, step, 0)
    if not last:
        put_ends(q_out, None, lo_out, hi_out)


def adjoint_kernel(moment, final, *refs):
    it = iter(refs)
    info, count, cells, which, traces = (next(it) for _ in range(5))
    a_now, b_now, a_old, b_old, stiff, stretch, lo, hi = (next(it) for _ in range(8))
    with_image = moment < 2
    if with_image:
        flat_in, deep_in, one_in, two_in = (next(it) for _ in range(4))
    if final:
        keep_out, send_out = next(it), next(it)
    else:
        a_out, b_out, lo_out, hi_out = (next(it) for _ in range(4))
        if with_image:
            one_out, two_out = next(it), next(it)
    ext = next(it)
    if final:
        a_out, b_out = next(it), next(it)
    depth, width, length = a_now.shape
    fill(ext, lo, hi)
    lanes = lax.broadcasted_iota(jnp.int32, (ROWS, length), 1)

    def weigh(layer, _):
        ext[layer + 2] = stiff[layer] * (a_now[layer] + b_now[layer])
        return 0

    lax.fori_loop(0, depth, weigh, 0)

    def step(layer, _):
        for start in range(0, width, ROWS):
            rows = pl.ds(start, ROWS)

            def weighted(s, n):
                r = pl.ds(s, n)
                return stiff[layer, r, :] * (stretch[layer, r, :] * a_now[layer, r, :] + b_now[layer, r, :])

            flat = lateral(edge_rows(weighted, start, width), lanes)
            deep = vertical(ext, layer, rows)
            a_out[layer, rows, :] = 2.0 * a_now[layer, rows, :] - a_old[layer, rows, :] + flat
            b_out[layer, rows, :] = 2.0 * b_now[layer, rows, :] - b_old[layer, rows, :] + deep
        return 0

    lax.fori_loop(0, depth, step, 0)
    tile_row = lax.broadcasted_iota(jnp.int32, (8, length), 0)
    tile_lane = lax.broadcasted_iota(jnp.int32, (8, length), 1)
    tile_place = tile_row * length + tile_lane

    def drop(n, _):
        cell = cells[n]
        tile = cell // (8 * length)
        layer = tile // (width // 8)
        rows = pl.ds(pl.multiple_of((tile % (width // 8)) * 8, 8), 8)
        add = jnp.where(tile_place == cell % (8 * length), traces[0, moment, which[n]], 0.0)
        a_out[layer, rows, :] = a_out[layer, rows, :] + add
        return 0

    lax.fori_loop(0, count[0], drop, 0)

    if with_image:
        core = info[2]

        def image(layer, _):
            for start in range(0, width, ROWS):
                rows = pl.ds(start, ROWS)
                a, b = a_out[layer, rows, :], b_out[layer, rows, :]
                flat, deep = flat_in[layer, rows, :], deep_in[layer, rows, :]
                one = one_in[layer, rows, :] + a * flat
                two = two_in[layer, rows, :] + a * deep + b * (flat + deep)
                if final:
                    keep_out[layer, rows, :] = jnp.where(core == 0, one, two)
                    send_out[layer, rows, :] = jnp.where(core == 0, two, one)
                else:
                    one_out[layer, rows, :] = one
                    two_out[layer, rows, :] = two
            return 0

        lax.fori_loop(0, depth, image, 0)
    if not final:
        for layer in range(2):
            lo_out[layer] = stiff[layer] * (a_out[layer] + b_out[layer])
            top = depth - 2 + layer
            hi_out[layer] = stiff[top] * (a_out[top] + b_out[top])


def receivers_kernel(info, receivers, count, cells, which):
    size = info[3]
    count[0] = 0

    def look(n, found):
        cell = receivers[0, n] - info[0]
        inside = (cell >= 0) & (cell < size)

        cells[found] = jnp.where(inside, cell, 0)
        which[found] = n
        return found + jnp.where(inside, 1, 0)

    count[0] = lax.fori_loop(0, receivers.shape[1], look, 0)


def quad_kernel(info, vel, eps, from_core, from_side, from_both, out):
    core, side = info[2], info[4]
    rows = vel.shape[1]
    mine = jnp.where(core == 0, vel[...], eps[...])
    for c in range(2):
        near = jnp.where(core == c, mine, from_core[...])
        far = jnp.where(core == c, from_side[...], from_both[...])
        out[:, rows * c : rows * (c + 1), :] = jnp.where(side == 0, near, far)
        out[:, rows * (2 + c) : rows * (3 + c), :] = jnp.where(side == 0, far, near)


def model_kernel(info, *refs):
    own, other = refs[0:9], refs[9:18]
    a_ref, b_ref, stiff, stretch, lo_out, hi_out = refs[18:]
    core, line = info[2], info[5]
    depth, width, length = stiff.shape
    band = own[0].shape[1]
    lines = width // band

    def place(steps):
        return pl.ds(pl.multiple_of(lax.rem(line + steps, lines) * band, band), band)

    steps = (0, 1, 7, 2, 6, 3, 5)
    pieces = [(own[i], other[i], place(s), 0) for i, s in enumerate(steps)]
    pieces += [(own[7], other[7], place(4), 0), (own[8], other[8], place(4), depth // 2)]
    for mine, theirs, rows, first in pieces:
        for layer in range(mine.shape[0]):
            x, y = mine[layer], theirs[layer]
            vel = jnp.where(core == 0, x, y)
            eps = jnp.where(core == 0, y, x)
            stiff[first + layer, rows, :] = vel * vel
            stretch[first + layer, rows, :] = 1.0 + 2.0 * eps
    for layer in range(2):
        lo_out[layer] = stiff[layer] * (a_ref[layer] + b_ref[layer])
        top = depth - 2 + layer
        hi_out[layer] = stiff[top] * (a_ref[top] + b_ref[top])


def split_kernel(info, keep, got, *outs):
    line = info[5]
    width = keep.shape[1]
    band = outs[0].shape[1]
    lines = width // band
    half = keep.shape[0] // 2
    for i, steps in enumerate((0, 1, 7, 2, 6, 3, 5)):
        rows = pl.ds(pl.multiple_of(lax.rem(line + steps, lines) * band, band), band)
        outs[i][...] = keep[:, rows, :] + got[:, rows, :]
    rows = pl.ds(pl.multiple_of(lax.rem(line + 4, lines) * band, band), band)
    outs[7][...] = keep[:half, rows, :] + got[:half, rows, :]
    outs[8][...] = keep[half:, rows, :] + got[half:, rows, :]


def relay_kernel(plus, minus, from_minus, from_plus, low, high, plus_out, minus_out):
    half = low.shape[0]
    plus_out[...] = plus[...] + from_minus[...]
    minus_out[...] = minus[...] + from_plus[...]
    plus_out[0:half] = plus_out[0:half] + low[...]
    minus_out[half:] = minus_out[half:] + high[...]


def lines_kernel(info, own, r1, r2, r3, r4, keep, send):
    side = info[4]
    total = (own[...] + (r1[...] + r2[...])) + (r3[...] + r4[...])
    rows = keep.shape[1]
    keep[...] = jnp.where(side == 0, total[:, :rows], total[:, rows:])
    send[...] = jnp.where(side == 0, total[:, rows:], total[:, :rows])


def sides_kernel(info, keep, got, mine, send):
    core = info[2]
    rows = mine.shape[1]
    low = keep[:, :rows, :] + got[:, :rows, :]
    high = keep[:, rows:, :] + got[:, rows:, :]
    mine[...] = jnp.where(core == 0, low, high)
    send[...] = jnp.where(core == 0, high, low)


def gradient_kernel(info, mine, got, vel, eps, vel_out, eps_out):
    core = info[2]
    one = jnp.where(core == 0, mine[...], got[...])
    two = jnp.where(core == 0, got[...], mine[...])
    v = vel[...]
    vel_out[...] = 2.0 * v * ((1.0 + 2.0 * eps[...]) * one + two)
    eps_out[...] = 2.0 * (v * v) * one


def on_device(
    velocity, epsilon, forward_state, adjoint_state, source_cell, wavelet, receiver_cells, residuals
):
    depth, share, length = velocity.shape
    width = forward_state.shape[3]
    shots = lax.axis_size("shot")
    slabs = lax.axis_size("dom")
    lines = shots // 4
    field = shape(depth, width, length)
    ends = shape(2, width, length)
    shot = lax.axis_index("shot")
    core, side, line = shot % 2, (shot // 2) % 2, shot // 4
    info = jnp.stack(
        [
            lax.axis_index("dom") * (depth * width * length),
            source_cell[0],
            core,
            jnp.int32(depth * width * length),
            side,
            line,
        ]
    ).astype(jnp.int32)

    up = [(i, i + 1) for i in range(slabs - 1)]
    down = [(i + 1, i) for i in range(slabs - 1)]

    def halos(lo, hi):
        return lax.ppermute(hi, "dom", up), lax.ppermute(lo, "dom", down)

    def swap(x, mask):
        return lax.ppermute(x, "shot", [(s, s ^ mask) for s in range(shots)])

    def from_line(x, steps):
        pairs = [(s, ((s // 4 - steps) % lines) * 4 + s % 4) for s in range(shots)]
        return lax.ppermute(x, "shot", pairs)

    p_old, p_now, q_old, q_now = (forward_state[0, i] for i in range(4))
    a_old, a_now, b_old, b_now = (adjoint_state[0, i] for i in range(4))

    mine = jnp.where(core == 0, velocity, epsilon)
    theirs = jnp.where(core == 0, epsilon, velocity)
    from_side = swap(mine, 2)
    from_both = swap(theirs, 3)
    from_core = swap(theirs, 1)
    q_lo, q_hi = halos(q_now[:2], q_now[depth - 2 :])
    quad = call(
        quad_kernel,
        [shape(depth, 4 * share, length)],
        (info, velocity, epsilon, from_core, from_side, from_both),
        1,
    )[0]
    half = depth // 2
    n2, m2 = from_line(quad, 2), from_line(quad, -2)
    n1, m1 = from_line(quad, 1), from_line(quad, -1)
    low, high = from_line(n2[:half], 2), from_line(m2[half:], -2)
    n3, m3 = from_line(n2, 1), from_line(m2, -1)
    own = (quad, n1, m1, n2, m2, n3, m3, low, high)
    other = tuple(swap(x, 1) for x in own)
    stiff, stretch, w_lo, w_hi = call(
        model_kernel, [field, field, ends, ends], (info, *own, *other, a_now, b_now), 1
    )
    spots = jax.ShapeDtypeStruct((receiver_cells.shape[1] + 1,), jnp.int32)
    count, cells, which = call(
        receivers_kernel,
        [jax.ShapeDtypeStruct((1,), jnp.int32), spots, spots],
        (info, receiver_cells),
        2,
        out_specs=[SMEM] * 3,
    )
    ext = pltpu.VMEM((depth + 4, width, length), jnp.float32)
    plane = pltpu.VMEM((depth, width, length), jnp.float32)

    def forward(moment, extra, with_image, last, outs):
        return call(
            functools.partial(forward_kernel, moment, with_image, last),
            outs,
            (info, wavelet, p_now, q_now, q_lo, q_hi, *extra),
            2,
            [ext],
        )

    def adjoint(moment, extra, final, outs):
        return call(
            functools.partial(adjoint_kernel, moment, final),
            outs,
            (info, count, cells, which, residuals, a_now, b_now, a_old, b_old, stiff, stretch, w_lo, w_hi, *extra),
            5,
            [ext] + ([plane, plane] if final else []),
        )

    six = [field, field, ends, ends, field, field]
    flats, deeps = [], []
    w_lo, w_hi = halos(w_lo, w_hi)
    p_new, q_new, lo, hi, flat, deep = forward(0, (p_old, q_old, stiff, stretch), False, False, six)
    flats.append(flat)
    deeps.append(deep)
    p_old, p_now, q_old, q_now = p_now, p_new, q_now, q_new
    q_lo, q_hi = halos(lo, hi)

    a_new, b_new, lo, hi = adjoint(3, (), False, six[:4])
    a_old, a_now, b_old, b_now = a_now, a_new, b_now, b_new
    a_four, b_four = a_new, b_new
    w_lo, w_hi = halos(lo, hi)

    p_new, q_new, lo, hi, flat, deep = forward(1, (p_old, q_old, stiff, stretch), False, False, six)
    flats.append(flat)
    deeps.append(deep)
    p_old, p_now, q_old, q_now = p_now, p_new, q_now, q_new
    q_lo, q_hi = halos(lo, hi)

    a_new, b_new, lo, hi = adjoint(2, (), False, six[:4])
    a_old, a_now, b_old, b_now = a_now, a_new, b_now, b_new
    w_lo, w_hi = halos(lo, hi)

    p_new, q_new, lo, hi, one, two = forward(2, (p_old, q_old, stiff, stretch, a_now, b_now), True, False, six)
    p_old, p_now, q_old, q_now = p_now, p_new, q_now, q_new
    q_lo, q_hi = halos(lo, hi)

    a_new, b_new, lo, hi, one, two = adjoint(1, (flats[1], deeps[1], one, two), False, six)
    a_old, a_now, b_old, b_now = a_now, a_new, b_now, b_new
    w_lo, w_hi = halos(lo, hi)

    one, two = forward(3, (a_four, b_four, one, two), True, True, [field, field])
    keep, send = adjoint(0, (flats[0], deeps[0], one, two), True, [field, field])

    band = shape(depth, 4 * share, length)
    half_band = shape(half, 4 * share, length)
    got = swap(send, 1)
    own, s1, t1, s2, t2, s3, t3, low, high = call(
        split_kernel, [band] * 7 + [half_band] * 2, (info, keep, got), 1
    )
    g3, h3 = from_line(s3, -1), from_line(t3, 1)
    g4, h4 = from_line(low, -2), from_line(high, 2)
    s2, t2 = call(relay_kernel, [band] * 2, (s2, t2, g3, h3, g4, h4))
    got = [from_line(s2, -2), from_line(t2, 2), from_line(s1, -1), from_line(t1, 1)]
    pair = shape(depth, 2 * share, length)
    keep, send = call(lines_kernel, [pair, pair], (info, own, *got), 1)
    keep, send = call(
        sides_kernel, [shape(depth, share, length)] * 2, (info, keep, swap(send, 2)), 1
    )
    vel_grad, eps_grad = call(
        gradient_kernel,
        [shape(depth, share, length)] * 2,
        (info, keep, swap(send, 1), velocity, epsilon),
        1,
    )
    return vel_grad, eps_grad


def solution(mesh):
    placed = (
        P("dom", "shot", None),
        P("dom", "shot", None),
        P("shot", None, "dom", None, None),
        P("shot", None, "dom", None, None),
        P("shot"),
        P("shot", None),
        P("shot", None),
        P("shot", None, None),
    )
    return jax.shard_map(
        on_device,
        mesh=mesh,
        in_specs=placed,
        out_specs=(P("dom", "shot", None), P("dom", "shot", None)),
        check_vma=False,
    )
```

```python
import functools

import jax
import jax.numpy as jnp
from jax import lax
from jax.experimental import pallas as pl
from jax.experimental.pallas import tpu as pltpu
from jax.sharding import PartitionSpec as P


ROWS, LANES = 32, 128
VMEM = pl.BlockSpec(memory_space=pltpu.VMEM)
SMEM = pl.BlockSpec(memory_space=pltpu.SMEM)


def shape(*dims):
    return jax.ShapeDtypeStruct(dims, jnp.float32)


def call(body, outs, args, scalars=0, scratch=(), out_specs=None, work=1.0, away=0):
    specs = [SMEM] * scalars + [VMEM] * (len(args) - scalars - away)
    specs += [pl.BlockSpec(memory_space=pltpu.HBM)] * away
    size = sum(4 * a.size for a in args) + sum(4 * o.size for o in outs)
    return pl.pallas_call(
        body,
        out_shape=tuple(outs),
        in_specs=specs,
        out_specs=tuple(out_specs or [VMEM] * len(outs)),
        scratch_shapes=list(scratch),
        compiler_params=pltpu.CompilerParams(vmem_limit_bytes=12 * 1024 * 1024),
        cost_estimate=pl.CostEstimate(
            flops=int(work * size * 4), bytes_accessed=size, transcendentals=0
        ),
    )(*args)


def edge_rows(load, start, count):
    parts = []
    low, high = max(start - 8, 0), min(start + ROWS + 8, count)
    body = load(low, high - low)
    blank = jnp.zeros((8, body.shape[1]), jnp.float32)
    if start == 0:
        parts.append(blank)
    parts.append(body)
    if start + ROWS == count:
        parts.append(blank)
    return jnp.concatenate(parts, axis=0) if len(parts) > 1 else body


def along_rows(wide, shift):
    return pltpu.roll(wide, shift % wide.shape[0], 0)[8 : 8 + ROWS]


def along_lanes(mid, lanes, shift):
    tiles = [mid[:, i : i + LANES] for i in range(0, mid.shape[1], LANES)]
    moved = [pltpu.roll(t, shift % LANES, 1) for t in tiles]
    out = []
    for i, own in enumerate(moved):
        j = i - 1 if shift > 0 else i + 1
        beside = moved[j] if 0 <= j < len(moved) else 0.0
        keep = lanes >= shift if shift > 0 else lanes < LANES + shift
        out.append(jnp.where(keep, own, beside))
    return jnp.concatenate(out, axis=1)


def lateral(wide, lanes):
    mid = wide[8 : 8 + ROWS]
    near = (along_rows(wide, 1) + along_rows(wide, -1)) + (
        along_lanes(mid, lanes, 1) + along_lanes(mid, lanes, -1)
    )
    far = (along_rows(wide, 2) + along_rows(wide, -2)) + (
        along_lanes(mid, lanes, 2) + along_lanes(mid, lanes, -2)
    )
    return 16.0 * near - far - 60.0 * mid


def vertical(ext, layer, rows):
    def at(offset):
        return ext[layer + offset, rows, :]

    return 16.0 * (at(1) + at(3)) - (at(0) + at(4)) - 30.0 * at(2)


def lane_index():
    return lax.broadcasted_iota(jnp.int32, (ROWS, LANES), 1)


def fill(ext, lo, hi):
    depth = ext.shape[0] - 4
    ext[0:2] = lo
    ext[depth + 2 : depth + 4] = hi


def put_ends(ref, lo_out, hi_out):
    depth = ref.shape[0]
    lo_out[...] = ref[0:2]
    hi_out[...] = ref[depth - 2 : depth]


def add_at(ref, cell, amount):
    _, width, length = ref.shape
    place = lax.broadcasted_iota(jnp.int32, (8, length), 0) * length
    place = place + lax.broadcasted_iota(jnp.int32, (8, length), 1)
    tile = cell // (8 * length)
    layer = tile // (width // 8)
    rows = pl.ds(pl.multiple_of((tile % (width // 8)) * 8, 8), 8)
    ref[layer, rows, :] = ref[layer, rows, :] + jnp.where(place == cell % (8 * length), amount, 0.0)


def forward_kernel(moment, *refs):
    it = iter(refs)
    info, pulse = next(it), next(it)
    state = next(it)
    if moment == 0:
        p_old, p_now, q_old, q_now = (state.at[0, i] for i in range(4))
    else:
        p_now, q_now = next(it), next(it)
        if moment == 1:
            p_old, q_old = state.at[0, 1], state.at[0, 3]
        else:
            p_old, q_old = state, next(it)
    stiff, stretch, lo, hi = (next(it) for _ in range(4))
    if moment == 2:
        back, side, one_in, two_in = (next(it) for _ in range(4))
    p_out, q_out = next(it), next(it)
    if moment < 2:
        lo_out, hi_out = next(it), next(it)
    first_out, second_out = next(it), next(it)
    ext = next(it)
    depth, width, _ = stiff.shape
    if moment == 0:
        fill(ext, lo[1], hi[1])
    else:
        fill(ext, lo[...], hi[...])
    lanes = lane_index()

    def copy(layer, _):
        ext[layer + 2] = q_now[layer]
        return 0

    lax.fori_loop(0, depth, copy, 0)

    def step(layer, _):
        for start in range(0, width, ROWS):
            rows = pl.ds(start, ROWS)
            flat = lateral(edge_rows(lambda s, n: p_now[layer, pl.ds(s, n), :], start, width), lanes)
            deep = vertical(ext, layer, rows)
            k = stiff[layer, rows, :]
            p_out[layer, rows, :] = (
                2.0 * p_now[layer, rows, :]
                - p_old[layer, rows, :]
                + k * (stretch[layer, rows, :] * flat + deep)
            )
            both = flat + deep
            q_out[layer, rows, :] = 2.0 * q_now[layer, rows, :] - q_old[layer, rows, :] + k * both
            if moment == 2:
                a, b = back[layer, rows, :], side[layer, rows, :]
                first_out[layer, rows, :] = one_in[layer, rows, :] + a * flat
                second_out[layer, rows, :] = two_in[layer, rows, :] + a * deep + b * both
            else:
                first_out[layer, rows, :] = flat
                second_out[layer, rows, :] = deep
        return 0

    lax.fori_loop(0, depth, step, 0)
    here = info[1] - info[0]

    @pl.when((here >= 0) & (here < info[3]))
    def _():
        add_at(p_out, here, pulse[0, moment])
        add_at(q_out, here, pulse[0, moment])

    if moment < 2:
        put_ends(q_out, lo_out, hi_out)


def last_kernel(p_now, q_now, back, side, one_in, two_in, lo, hi, one_out, two_out, lo_out, hi_out, ext):
    depth, width, length = p_now.shape
    zero = jnp.zeros((2, width, length), jnp.float32)
    fill(ext, zero, zero)
    lanes = lane_index()

    def copy(layer, _):
        ext[layer + 2] = q_now[layer]
        return 0

    lax.fori_loop(0, depth, copy, 0)

    def step(layer, _):
        for start in range(0, width, ROWS):
            rows = pl.ds(start, ROWS)
            flat = lateral(edge_rows(lambda s, n: p_now[layer, pl.ds(s, n), :], start, width), lanes)
            deep = vertical(ext, layer, rows)
            a, b = back[layer, rows, :], side[layer, rows, :]
            one_out[layer, rows, :] = one_in[layer, rows, :] + a * flat
            two_out[layer, rows, :] = two_in[layer, rows, :] + (a + b) * deep + b * flat
        return 0

    lax.fori_loop(0, depth, step, 0)
    lo_out[0] = -lo[0] * q_now[0]
    lo_out[1] = lo[1] * (16.0 * q_now[0] - q_now[1])
    hi_out[0] = hi[0] * (16.0 * q_now[depth - 1] - q_now[depth - 2])
    hi_out[1] = -hi[1] * q_now[depth - 1]


def adjoint_kernel(moment, *refs):
    it = iter(refs)
    _, count, cells, which, traces = (next(it) for _ in range(5))
    state = next(it)
    if moment == 3:
        a_old, a_now, b_old, b_now = (state.at[0, i] for i in range(4))
    else:
        a_now, b_now = next(it), next(it)
        if moment == 2:
            a_old, b_old = state.at[0, 1], state.at[0, 3]
        else:
            a_old, b_old = state, next(it)
    stiff, stretch = next(it), next(it)
    if moment > 1:
        lo, hi = next(it), next(it)
        a_out, b_out, lo_out, hi_out = (next(it) for _ in range(4))
    else:
        flat_in, deep_in = next(it), next(it)
        a_out, b_out, one_out, two_out = (next(it) for _ in range(4))
    ext = next(it)
    depth, width, length = stiff.shape
    if moment > 1:
        fill(ext, lo[...], hi[...])
    else:
        zero = jnp.zeros((2, width, length), jnp.float32)
        fill(ext, zero, zero)
    lanes = lane_index()

    def weigh(layer, _):
        ext[layer + 2] = stiff[layer] * (a_now[layer] + b_now[layer])
        return 0

    lax.fori_loop(0, depth, weigh, 0)

    def step(layer, _):
        for start in range(0, width, ROWS):
            rows = pl.ds(start, ROWS)

            def weighted(s, n):
                r = pl.ds(s, n)
                return stiff[layer, r, :] * (stretch[layer, r, :] * a_now[layer, r, :] + b_now[layer, r, :])

            flat = lateral(edge_rows(weighted, start, width), lanes)
            deep = vertical(ext, layer, rows)
            a_out[layer, rows, :] = 2.0 * a_now[layer, rows, :] - a_old[layer, rows, :] + flat
            b_out[layer, rows, :] = 2.0 * b_now[layer, rows, :] - b_old[layer, rows, :] + deep
        return 0

    lax.fori_loop(0, depth, step, 0)

    def drop(n, _):
        add_at(a_out, cells[n], traces[0, moment, which[n]])
        return 0

    lax.fori_loop(0, count[0], drop, 0)

    if moment > 1:
        for layer in range(2):
            lo_out[layer] = stiff[layer] * (a_out[layer] + b_out[layer])
            top = depth - 2 + layer
            hi_out[layer] = stiff[top] * (a_out[top] + b_out[top])
        return

    def image(layer, _):
        for start in range(0, width, ROWS):
            rows = pl.ds(start, ROWS)
            a, b = a_out[layer, rows, :], b_out[layer, rows, :]
            flat, deep = flat_in[layer, rows, :], deep_in[layer, rows, :]
            one_out[layer, rows, :] = a * flat
            two_out[layer, rows, :] = (a + b) * deep + b * flat
        return 0

    lax.fori_loop(0, depth, image, 0)


def final_kernel(*refs):
    info, count, cells, which, traces, pulse = refs[:6]
    a_now, b_part, a_old, b_old, stiff, stretch, lo, hi = refs[6:14]
    flat_two, deep_two, flat_in, deep_in, one_in, two_in = refs[14:20]
    lo_first, hi_first, lo_next, hi_next, lo_share, hi_share = refs[20:26]
    keep_out, send_out, ext, b_now, a_out, move = refs[26:]
    core = info[2]
    depth, width, length = stiff.shape
    zero = jnp.zeros((2, width, length), jnp.float32)
    fill(ext, zero, zero)
    lanes = lane_index()

    def fix(layer):
        if layer == 0:
            return 16.0 * lo[1] - lo[0]
        if layer == 1:
            return -lo[1]
        if layer == depth - 1:
            return 16.0 * hi[0] - hi[1]
        return -hi[0]

    ends = (0, 1, depth - 2, depth - 1)
    for n, layer in enumerate(ends):
        move[n] = fix(layer)
        b_now[layer] = b_part[layer] + move[n]

    def inner(layer, _):
        b_now[layer] = b_part[layer]
        return 0

    lax.fori_loop(2, depth - 2, inner, 0)

    def weigh(layer, _):
        ext[layer + 2] = stiff[layer] * (a_now[layer] + b_now[layer])
        return 0

    lax.fori_loop(0, depth, weigh, 0)

    def step(layer, _):
        for start in range(0, width, ROWS):
            rows = pl.ds(start, ROWS)

            def weighted(s, n):
                r = pl.ds(s, n)
                return stiff[layer, r, :] * (stretch[layer, r, :] * a_now[layer, r, :] + b_now[layer, r, :])

            flat = lateral(edge_rows(weighted, start, width), lanes)
            a_out[layer, rows, :] = 2.0 * a_now[layer, rows, :] - a_old[layer, rows, :] + flat
        return 0

    lax.fori_loop(0, depth, step, 0)

    def drop(n, _):
        add_at(a_out, cells[n], traces[0, 0, which[n]])
        return 0

    lax.fori_loop(0, count[0], drop, 0)

    def image(layer, _):
        for start in range(0, width, ROWS):
            rows = pl.ds(start, ROWS)
            a = a_out[layer, rows, :]
            b = 2.0 * b_now[layer, rows, :] - b_old[layer, rows, :] + vertical(ext, layer, rows)
            flat, deep = flat_in[layer, rows, :], deep_in[layer, rows, :]
            one = one_in[layer, rows, :] + a * flat
            two = two_in[layer, rows, :] + (a + b) * deep + b * flat

            @pl.when(core == 0)
            def _():
                keep_out[layer, rows, :] = one
                send_out[layer + 2, rows, :] = two

            @pl.when(core != 0)
            def _():
                send_out[layer, rows, :] = one
                keep_out[layer + 2, rows, :] = two

        return 0

    lax.fori_loop(0, depth, image, 0)
    gain = a_out
    gain[0:2] = lo_next[...] - 2.0 * lo_first[1] + lo_first[0]
    gain[2:4] = hi_next[...] - 2.0 * hi_first[1] + hi_first[0]
    plane = width * length
    here = info[1] - info[0]

    @pl.when((here >= -2 * plane) & (here < 0))
    def _():
        add_at(gain, here + 2 * plane, -pulse[0, 0])

    @pl.when((here >= depth * plane) & (here < (depth + 2) * plane))
    def _():
        add_at(gain, here - (depth - 2) * plane, -pulse[0, 0])

    def w(layer):
        return ext[layer + 2]

    low = (
        lo_share[0] - w(0) * gain[0],
        lo_share[1] + (16.0 * w(0) - w(1)) * gain[1],
    )
    high = (
        hi_share[0] + (16.0 * w(depth - 1) - w(depth - 2)) * gain[2],
        hi_share[1] - w(depth - 1) * gain[3],
    )
    change = [move[n] * (flat_two[l] + deep_two[l]) for n, l in enumerate(ends)]

    def finish(first, second):
        for n in range(2):
            first[depth + n] = low[n]
            second[n] = high[n]
        for n, l in enumerate(ends):
            second[l + 2] = second[l + 2] + change[n]

    @pl.when(core == 0)
    def _():
        finish(keep_out, send_out)

    @pl.when(core != 0)
    def _():
        finish(send_out, keep_out)


def receivers_kernel(info, receivers, count, cells, which):
    size = info[3]
    count[0] = 0

    def look(n, found):
        cell = receivers[0, n] - info[0]
        inside = (cell >= 0) & (cell < size)

        cells[found] = jnp.where(inside, cell, 0)
        which[found] = n
        return found + jnp.where(inside, 1, 0)

    count[0] = lax.fori_loop(0, receivers.shape[1], look, 0, unroll=8)


def quad_kernel(info, own, from_core, from_side, from_both, out):
    core, side = info[2], info[4]
    rows = own.shape[1]
    mine = own[...]
    for c in range(2):
        near = jnp.where(core == c, mine, from_core[...])
        far = jnp.where(core == c, from_side[...], from_both[...])
        out[:, rows * c : rows * (c + 1), :] = jnp.where(side == 0, near, far)
        out[:, rows * (2 + c) : rows * (3 + c), :] = jnp.where(side == 0, far, near)


def model_kernel(pieces, info, count, *refs):
    size = len(pieces)
    own, other = refs[:size], refs[size : 2 * size]
    low, high, stiff, stretch, lo_out, hi_out = refs[2 * size :]
    core, line = info[2], info[5]
    _, width, _ = stiff.shape
    band = own[0].shape[1]
    lines = width // band
    for mine, theirs, (steps, first) in zip(own, other, pieces):
        rows = pl.ds(pl.multiple_of(lax.rem(line + steps, lines) * band, band), band)
        for i in range(mine.shape[0]):
            layer = first + i - 2
            x, y = mine[i], theirs[i]
            vel = jnp.where(core == 0, x, y)
            rest = jnp.where(core == 0, y, x)
            k = vel * vel * (1.0 / 12.0)
            if layer < 0:
                lo_out[layer + 2, rows, :] = k * low[layer + 2, rows, :]
                above = rest * rest * (1.0 / 12.0)
                hi_out[layer + 2, rows, :] = above * high[layer + 2, rows, :]
            else:
                stiff[layer, rows, :] = k
                stretch[layer, rows, :] = 1.0 + 2.0 * rest


def split_kernel(info, keep, got, *outs):
    line = info[5]
    width = keep.shape[1]
    band = outs[0].shape[1]
    lines = width // band
    half = keep.shape[0] // 2
    for i, steps in enumerate((0, 1, 7, 2, 6, 3, 5)):
        rows = pl.ds(pl.multiple_of(lax.rem(line + steps, lines) * band, band), band)
        outs[i][...] = keep[:, rows, :] + got[:, rows, :]
    rows = pl.ds(pl.multiple_of(lax.rem(line + 4, lines) * band, band), band)
    outs[7][...] = keep[:half, rows, :] + got[:half, rows, :]
    outs[8][...] = keep[half:, rows, :] + got[half:, rows, :]


def relay_kernel(plus, minus, from_minus, from_plus, low, high, plus_out, minus_out):
    half = low.shape[0]
    plus_out[...] = plus[...] + from_minus[...]
    minus_out[...] = minus[...] + from_plus[...]
    plus_out[0:half] = plus_out[0:half] + low[...]
    minus_out[half:] = minus_out[half:] + high[...]


def lines_kernel(info, own, r1, r2, r3, r4, keep, send, straight, across):
    core, side = info[2], info[4]
    total = (own[...] + (r1[...] + r2[...])) + (r3[...] + r4[...])
    layers, rows, _ = keep.shape
    near = jnp.where(side == 0, total[:, :rows], total[:, rows:])
    far = jnp.where(side == 0, total[:, rows:], total[:, :rows])
    keep[...] = near
    send[...] = far
    straight[...] = jnp.where(core == 0, near[layers - 2 :], near[:2])
    across[...] = jnp.where(core == 0, far[layers - 2 :], far[:2])


def sides_kernel(info, keep, got, straight, across, mine, send):
    core = info[2]
    layers, width, _ = keep.shape
    rows = width // 2

    def place(first, count, total):
        low, high = total[:, :rows, :], total[:, rows:, :]
        mine[first : first + count] = jnp.where(core == 0, low, high)
        send[first : first + count] = jnp.where(core == 0, high, low)

    place(0, layers, keep[...] + got[...])
    place(layers, 2, straight[...] + across[...])


def gradient_kernel(info, mine, got, vel, eps, vel_out, eps_out):
    core = info[2]
    depth = vel.shape[0]
    one = jnp.where(core == 0, mine[:depth], got[:depth]) * (1.0 / 12.0)
    two = jnp.where(core == 0, got[2 : depth + 2], mine[2 : depth + 2]) * (1.0 / 12.0)
    from_above = jnp.where(core == 0, mine[depth + 2 :], got[depth + 2 :])
    from_below = jnp.where(core == 0, got[depth + 2 :], mine[depth + 2 :])
    v = vel[...]
    stiff = v * v
    vel_out[...] = 2.0 * v * ((1.0 + 2.0 * eps[...]) * one + two)
    for layer in range(2):
        top = depth - 2 + layer
        vel_out[layer] = vel_out[layer] + 2.0 * v[layer] * (from_below[layer] / stiff[layer])
        vel_out[top] = vel_out[top] + 2.0 * v[top] * (from_above[layer] / stiff[top])
    eps_out[...] = 2.0 * stiff * one


def on_device(
    velocity, epsilon, forward_state, adjoint_state, source_cell, wavelet, receiver_cells, residuals
):
    depth, share, length = velocity.shape
    width = forward_state.shape[3]
    shots = lax.axis_size("shot")
    slabs = lax.axis_size("dom")
    lines = shots // 4
    field = shape(depth, width, length)
    ends = shape(2, width, length)
    shot = lax.axis_index("shot")
    core, side, line = shot % 2, (shot // 2) % 2, shot // 4
    info = jnp.stack(
        [
            lax.axis_index("dom") * (depth * width * length),
            source_cell[0],
            core,
            jnp.int32(depth * width * length),
            side,
            line,
        ]
    ).astype(jnp.int32)

    up = [(i, i + 1) for i in range(slabs - 1)]
    down = [(i + 1, i) for i in range(slabs - 1)]

    def halos(lo, hi):
        return lax.ppermute(hi, "dom", up), lax.ppermute(lo, "dom", down)

    def swap(x, mask):
        return lax.ppermute(x, "shot", [(s, s ^ mask) for s in range(shots)])

    def from_line(x, steps):
        pairs = [(s, ((s // 4 - steps) % lines) * 4 + s % 4) for s in range(shots)]
        return lax.ppermute(x, "shot", pairs)

    below, above = halos(velocity[:2], velocity[depth - 2 :])
    first_part = jnp.concatenate([below, velocity], axis=0)
    second_part = jnp.concatenate([above, epsilon], axis=0)
    mine = jnp.where(core == 0, first_part, second_part)
    theirs = jnp.where(core == 0, second_part, first_part)
    from_side = swap(mine, 2)
    from_both = swap(theirs, 3)
    from_core = swap(theirs, 1)
    low_end, high_end = (
        jnp.concatenate(
            [forward_state[0, 2:4, rows], adjoint_state[0, 1:2, rows] + adjoint_state[0, 3:4, rows]], axis=0
        )
        for rows in (slice(0, 2), slice(depth - 2, depth))
    )
    q_lo, q_hi = halos(low_end, high_end)
    quad = call(
        quad_kernel,
        [shape(depth + 2, 4 * share, length)],
        (info, mine, from_core, from_side, from_both),
        1,
    )[0]
    half = depth // 2 + 1
    n2, m2 = from_line(quad, 2), from_line(quad, -2)
    n1, m1 = from_line(quad, 1), from_line(quad, -1)
    n3, m3 = from_line(n2, 1), from_line(m2, -1)
    low, high = from_line(n2[:half], 2), from_line(m2[half:], -2)
    blocks = (quad, n1, m1, n2, m2, n3, m3, low, high)
    pieces = ((0, 0), (1, 0), (7, 0), (2, 0), (6, 0), (3, 0), (5, 0), (4, 0), (4, half))
    other = tuple(swap(x, 1) for x in blocks)
    spots = jax.ShapeDtypeStruct((receiver_cells.shape[1] + 1,), jnp.int32)
    found = call(
        receivers_kernel,
        [jax.ShapeDtypeStruct((1,), jnp.int32), spots, spots],
        (info, receiver_cells),
        2,
        out_specs=[SMEM] * 3,
    )
    stiff, stretch, w_lo, w_hi = call(
        functools.partial(model_kernel, pieces),
        [field, field, ends, ends],
        (info, found[0], *blocks, *other, q_lo[2], q_hi[2]),
        2,
    )
    ext = pltpu.VMEM((depth + 4, width, length), jnp.float32)
    plane = pltpu.VMEM((depth, width, length), jnp.float32)
    model = (stiff, stretch)

    def forward(moment, outs, *args):
        body = functools.partial(forward_kernel, moment)
        return call(body, outs, (info, wavelet, *args), 2, [ext])

    def adjoint(moment, outs, *args):
        body = functools.partial(adjoint_kernel, moment)
        return call(body, outs, (info, *found, residuals, *args), 5, [ext])

    six = [field, field, ends, ends, field, field]
    p2, q2, lo, hi, flat1, deep1 = forward(0, six, forward_state, *model, q_lo, q_hi)
    q2_lo, q2_hi = halos(lo, hi)
    a4, b4, lo, hi = adjoint(3, six[:4], adjoint_state, *model, w_lo, w_hi)
    w3_lo, w3_hi = halos(lo, hi)
    p3, q3, lo, hi, flat2, deep2 = forward(1, six, forward_state, p2, q2, *model, q2_lo, q2_hi)
    q3_lo, q3_hi = halos(lo, hi)
    a3, b3, lo, hi = adjoint(2, six[:4], adjoint_state, a4, b4, *model, w3_lo, w3_hi)
    w2_lo, w2_hi = halos(lo, hi)
    a2, b2, one, two = adjoint(1, [field] * 4, a4, a3, b3, b4, *model, flat2, deep2)
    p4, q4, one, two = forward(2, [field] * 4, p2, p3, q3, q2, *model, q3_lo, q3_hi, a3, b3, one, two)
    one, two, lo_share, hi_share = call(
        last_kernel,
        [field, field, ends, ends],
        (p4, q4, a4, b4, one, two, w3_lo, w3_hi),
        0,
        [ext],
    )
    parts = shape(depth + 2, width, length)
    keep, send = call(
        final_kernel,
        [parts, parts],
        (info, *found, residuals, wavelet, a2, b2, a3, b3, *model, w2_lo, w2_hi)
        + (flat2, deep2, flat1, deep1, one, two, q_lo, q_hi, q2_lo, q2_hi, lo_share, hi_share),
        6,
        [ext, plane, plane, pltpu.VMEM((4, width, length), jnp.float32)],
    )

    band = shape(depth + 2, 4 * share, length)
    half_band = shape(half, 4 * share, length)
    got = swap(send, 1)
    own, s1, t1, s2, t2, s3, t3, low, high = call(
        split_kernel, [band] * 7 + [half_band] * 2, (info, keep, got), 1
    )
    g3, h3 = from_line(s3, -1), from_line(t3, 1)
    g4, h4 = from_line(low, -2), from_line(high, 2)
    s2, t2 = call(relay_kernel, [band] * 2, (s2, t2, g3, h3, g4, h4))
    got = [from_line(s2, -2), from_line(t2, 2), from_line(s1, -1), from_line(t1, 1)]

    def to_slab(x, mask):
        pairs = []
        for s in range(shots):
            for d in range(slabs):
                target = d - 1 if s % 2 == 0 else d + 1
                if 0 <= target < slabs:
                    pairs.append((s * slabs + d, (s ^ mask) * slabs + target))
        return lax.ppermute(x, ("shot", "dom"), pairs)

    pair, rest = shape(depth + 2, 2 * share, length), shape(2, 2 * share, length)
    keep, send, straight, across = call(lines_kernel, [pair, pair, rest, rest], (info, own, *got), 1)
    quarter = shape(depth + 4, share, length)
    keep, send = call(
        sides_kernel,
        [quarter, quarter],
        (info, keep, swap(send, 2), to_slab(straight, 0), to_slab(across, 2)),
        1,
    )
    vel_grad, eps_grad = call(
        gradient_kernel,
        [shape(depth, share, length)] * 2,
        (info, keep, swap(send, 1), velocity, epsilon),
        1,
    )
    return vel_grad, eps_grad


def solution(mesh):
    placed = (
        P("dom", "shot", None),
        P("dom", "shot", None),
        P("shot", None, "dom", None, None),
        P("shot", None, "dom", None, None),
        P("shot"),
        P("shot", None),
        P("shot", None),
        P("shot", None, None),
    )

    return jax.shard_map(
        on_device,
        mesh=mesh,
        in_specs=placed,
        out_specs=(P("dom", "shot", None), P("dom", "shot", None)),
        check_vma=False,
    )
```

```python
import functools

import jax
import jax.numpy as jnp
from jax import lax
from jax.experimental import pallas as pl
from jax.experimental.pallas import tpu as pltpu
from jax.sharding import PartitionSpec as P


ROWS, LANES = 32, 128
VMEM = pl.BlockSpec(memory_space=pltpu.VMEM)
SMEM = pl.BlockSpec(memory_space=pltpu.SMEM)


def shape(*dims):
    return jax.ShapeDtypeStruct(dims, jnp.float32)


def call(body, outs, args, scalars=0, scratch=(), out_specs=None, work=1.0, away=0):
    specs = [SMEM] * scalars + [VMEM] * (len(args) - scalars - away)
    specs += [pl.BlockSpec(memory_space=pltpu.HBM)] * away
    size = sum(4 * a.size for a in args) + sum(4 * o.size for o in outs)
    return pl.pallas_call(
        body,
        out_shape=tuple(outs),
        in_specs=specs,
        out_specs=tuple(out_specs or [VMEM] * len(outs)),
        scratch_shapes=list(scratch),
        compiler_params=pltpu.CompilerParams(vmem_limit_bytes=12 * 1024 * 1024),
        cost_estimate=pl.CostEstimate(
            flops=int(work * size * 4), bytes_accessed=size, transcendentals=0
        ),
    )(*args)


def edge_rows(load, start, count):
    parts = []
    low, high = max(start - 8, 0), min(start + ROWS + 8, count)
    body = load(low, high - low)
    blank = jnp.zeros((8, body.shape[1]), jnp.float32)
    if start == 0:
        parts.append(blank)
    parts.append(body)
    if start + ROWS == count:
        parts.append(blank)
    return jnp.concatenate(parts, axis=0) if len(parts) > 1 else body


def along_rows(wide, shift):
    return pltpu.roll(wide, shift % wide.shape[0], 0)[8 : 8 + ROWS]


def along_lanes(mid, lanes, shift):
    tiles = [mid[:, i : i + LANES] for i in range(0, mid.shape[1], LANES)]
    moved = [pltpu.roll(t, shift % LANES, 1) for t in tiles]
    out = []
    for i, own in enumerate(moved):
        j = i - 1 if shift > 0 else i + 1
        beside = moved[j] if 0 <= j < len(moved) else 0.0
        keep = lanes >= shift if shift > 0 else lanes < LANES + shift
        out.append(jnp.where(keep, own, beside))
    return jnp.concatenate(out, axis=1)


def lateral(wide, lanes):
    mid = wide[8 : 8 + ROWS]
    near = (along_rows(wide, 1) + along_rows(wide, -1)) + (
        along_lanes(mid, lanes, 1) + along_lanes(mid, lanes, -1)
    )
    far = (along_rows(wide, 2) + along_rows(wide, -2)) + (
        along_lanes(mid, lanes, 2) + along_lanes(mid, lanes, -2)
    )
    return 16.0 * near - far - 60.0 * mid


def vertical(ext, layer, rows):
    def at(offset):
        return ext[layer + offset, rows, :]

    return 16.0 * (at(1) + at(3)) - (at(0) + at(4)) - 30.0 * at(2)


def lane_index():
    return lax.broadcasted_iota(jnp.int32, (ROWS, LANES), 1)


def fill(ext, lo, hi):
    depth = ext.shape[0] - 4
    ext[0:2] = lo
    ext[depth + 2 : depth + 4] = hi


def put_ends(ref, lo_out, hi_out):
    depth = ref.shape[0]
    lo_out[...] = ref[0:2]
    hi_out[...] = ref[depth - 2 : depth]


def add_at(ref, cell, amount):
    _, width, length = ref.shape
    place = lax.broadcasted_iota(jnp.int32, (8, length), 0) * length
    place = place + lax.broadcasted_iota(jnp.int32, (8, length), 1)
    tile = cell // (8 * length)
    layer = tile // (width // 8)
    rows = pl.ds(pl.multiple_of((tile % (width // 8)) * 8, 8), 8)
    ref[layer, rows, :] = ref[layer, rows, :] + jnp.where(place == cell % (8 * length), amount, 0.0)


def forward_kernel(moment, *refs):
    it = iter(refs)
    info, pulse = next(it), next(it)
    state = next(it)
    if moment == 0:
        p_old, p_now, q_old, q_now = (state.at[0, i] for i in range(4))
    else:
        p_now, q_now = next(it), next(it)
        if moment == 1:
            p_old, q_old = state.at[0, 1], state.at[0, 3]
        else:
            p_old, q_old = state, next(it)
    stiff, stretch, lo, hi = (next(it) for _ in range(4))
    if moment == 2:
        back, side, one_in, two_in = (next(it) for _ in range(4))
    p_out, q_out = next(it), next(it)
    if moment < 2:
        lo_out, hi_out = next(it), next(it)
    first_out, second_out = next(it), next(it)
    ext = next(it)
    depth, width, _ = stiff.shape
    if moment == 0:
        fill(ext, lo[1], hi[1])
    else:
        fill(ext, lo[...], hi[...])
    lanes = lane_index()

    def copy(layer, _):
        ext[layer + 2] = q_now[layer]
        return 0

    lax.fori_loop(0, depth, copy, 0)

    def step(layer, _):
        for start in range(0, width, ROWS):
            rows = pl.ds(start, ROWS)
            flat = lateral(edge_rows(lambda s, n: p_now[layer, pl.ds(s, n), :], start, width), lanes)
            deep = vertical(ext, layer, rows)
            k = stiff[layer, rows, :]
            p_out[layer, rows, :] = (
                2.0 * p_now[layer, rows, :]
                - p_old[layer, rows, :]
                + k * (stretch[layer, rows, :] * flat + deep)
            )
            both = flat + deep
            q_out[layer, rows, :] = 2.0 * q_now[layer, rows, :] - q_old[layer, rows, :] + k * both
            if moment == 2:
                a, b = back[layer, rows, :], side[layer, rows, :]
                first_out[layer, rows, :] = one_in[layer, rows, :] + a * flat
                second_out[layer, rows, :] = two_in[layer, rows, :] + a * deep + b * both
            else:
                first_out[layer, rows, :] = flat
                second_out[layer, rows, :] = deep
        return 0

    lax.fori_loop(0, depth, step, 0)
    here = info[1] - info[0]

    @pl.when((here >= 0) & (here < info[3]))
    def _():
        add_at(p_out, here, pulse[0, moment])
        add_at(q_out, here, pulse[0, moment])

    if moment < 2:
        put_ends(q_out, lo_out, hi_out)


def last_kernel(p_now, q_now, back, side, one_in, two_in, lo, hi, one_out, two_out, lo_out, hi_out, ext):
    depth, width, length = p_now.shape
    zero = jnp.zeros((2, width, length), jnp.float32)
    fill(ext, zero, zero)
    lanes = lane_index()

    def copy(layer, _):
        ext[layer + 2] = q_now[layer]
        return 0

    lax.fori_loop(0, depth, copy, 0)

    def step(layer, _):
        for start in range(0, width, ROWS):
            rows = pl.ds(start, ROWS)
            flat = lateral(edge_rows(lambda s, n: p_now[layer, pl.ds(s, n), :], start, width), lanes)
            deep = vertical(ext, layer, rows)
            a, b = back[layer, rows, :], side[layer, rows, :]
            one_out[layer, rows, :] = one_in[layer, rows, :] + a * flat
            two_out[layer, rows, :] = two_in[layer, rows, :] + (a + b) * deep + b * flat
        return 0

    lax.fori_loop(0, depth, step, 0)
    lo_out[0] = -lo[0] * q_now[0]
    lo_out[1] = lo[1] * (16.0 * q_now[0] - q_now[1])
    hi_out[0] = hi[0] * (16.0 * q_now[depth - 1] - q_now[depth - 2])
    hi_out[1] = -hi[1] * q_now[depth - 1]


def adjoint_kernel(moment, *refs):
    it = iter(refs)
    _, count, cells, which, traces = (next(it) for _ in range(5))
    state = next(it)
    if moment == 3:
        a_old, a_now, b_old, b_now = (state.at[0, i] for i in range(4))
    else:
        a_now, b_now = next(it), next(it)
        if moment == 2:
            a_old, b_old = state.at[0, 1], state.at[0, 3]
        else:
            a_old, b_old = state, next(it)
    stiff, stretch = next(it), next(it)
    if moment > 1:
        lo, hi = next(it), next(it)
        a_out, b_out, lo_out, hi_out = (next(it) for _ in range(4))
    else:
        flat_in, deep_in = next(it), next(it)
        a_out, b_out, one_out, two_out = (next(it) for _ in range(4))
    ext = next(it)
    depth, width, length = stiff.shape
    if moment > 1:
        fill(ext, lo[...], hi[...])
    else:
        zero = jnp.zeros((2, width, length), jnp.float32)
        fill(ext, zero, zero)
    lanes = lane_index()

    def weigh(layer, _):
        ext[layer + 2] = stiff[layer] * (a_now[layer] + b_now[layer])
        return 0

    lax.fori_loop(0, depth, weigh, 0)

    def step(layer, _):
        for start in range(0, width, ROWS):
            rows = pl.ds(start, ROWS)

            def weighted(s, n):
                r = pl.ds(s, n)
                return stiff[layer, r, :] * (stretch[layer, r, :] * a_now[layer, r, :] + b_now[layer, r, :])

            flat = lateral(edge_rows(weighted, start, width), lanes)
            deep = vertical(ext, layer, rows)
            a_out[layer, rows, :] = 2.0 * a_now[layer, rows, :] - a_old[layer, rows, :] + flat
            b_out[layer, rows, :] = 2.0 * b_now[layer, rows, :] - b_old[layer, rows, :] + deep
        return 0

    lax.fori_loop(0, depth, step, 0)

    def drop(n, _):
        add_at(a_out, cells[n], traces[0, moment, which[n]])
        return 0

    lax.fori_loop(0, count[0], drop, 0)

    if moment > 1:
        for layer in range(2):
            lo_out[layer] = stiff[layer] * (a_out[layer] + b_out[layer])
            top = depth - 2 + layer
            hi_out[layer] = stiff[top] * (a_out[top] + b_out[top])
        return

    def image(layer, _):
        for start in range(0, width, ROWS):
            rows = pl.ds(start, ROWS)
            a, b = a_out[layer, rows, :], b_out[layer, rows, :]
            flat, deep = flat_in[layer, rows, :], deep_in[layer, rows, :]
            one_out[layer, rows, :] = a * flat
            two_out[layer, rows, :] = (a + b) * deep + b * flat
        return 0

    lax.fori_loop(0, depth, image, 0)


def adjoint_rows(layer, start, a_now, b_now, a_old, stiff, stretch, lanes):
    def weighted(s, n):
        r = pl.ds(s, n)
        return stiff[layer, r, :] * (stretch[layer, r, :] * a_now[layer, r, :] + b_now[layer, r, :])

    rows = pl.ds(start, ROWS)
    flat = lateral(edge_rows(weighted, start, a_now.shape[1]), lanes)
    return 2.0 * a_now[layer, rows, :] - a_old[layer, rows, :] + flat


def inner_kernel(a_now, b_now, a_old, stiff, stretch, out):
    depth, width, _ = stiff.shape
    lanes = lane_index()

    def step(layer, _):
        for start in range(0, width, ROWS):
            rows = pl.ds(start, ROWS)
            out[layer - 2, rows, :] = adjoint_rows(layer, start, a_now, b_now, a_old, stiff, stretch, lanes)
        return 0

    lax.fori_loop(2, depth - 2, step, 0)


def final_kernel(*refs):
    info, count, cells, which, traces, pulse = refs[:6]
    a_now, b_part, a_old, b_old, stiff, stretch, lo, hi = refs[6:14]
    flat_two, deep_two, flat_in, deep_in, one_in, two_in = refs[14:20]
    lo_first, hi_first, lo_next, hi_next, lo_share, hi_share, middle = refs[20:27]
    keep_out, send_out, ext, b_now, a_out, move = refs[27:]
    core = info[2]
    depth, width, length = stiff.shape
    zero = jnp.zeros((2, width, length), jnp.float32)
    fill(ext, zero, zero)
    lanes = lane_index()

    def fix(layer):
        if layer == 0:
            return 16.0 * lo[1] - lo[0]
        if layer == 1:
            return -lo[1]
        if layer == depth - 1:
            return 16.0 * hi[0] - hi[1]
        return -hi[0]

    ends = (0, 1, depth - 2, depth - 1)
    for n, layer in enumerate(ends):
        move[n] = fix(layer)
        b_now[layer] = b_part[layer] + move[n]

    def inner(layer, _):
        b_now[layer] = b_part[layer]
        a_out[layer] = middle[layer - 2]
        return 0

    lax.fori_loop(2, depth - 2, inner, 0)

    def weigh(layer, _):
        ext[layer + 2] = stiff[layer] * (a_now[layer] + b_now[layer])
        return 0

    lax.fori_loop(0, depth, weigh, 0)

    def step(n, _):
        layer = jnp.where(n < 2, n, n + depth - 4)
        for start in range(0, width, ROWS):
            rows = pl.ds(start, ROWS)
            a_out[layer, rows, :] = adjoint_rows(layer, start, a_now, b_now, a_old, stiff, stretch, lanes)
        return 0

    lax.fori_loop(0, 4, step, 0)

    def drop(n, _):
        add_at(a_out, cells[n], traces[0, 0, which[n]])
        return 0

    lax.fori_loop(0, count[0], drop, 0)

    def image(layer, _):
        for start in range(0, width, ROWS):
            rows = pl.ds(start, ROWS)
            a = a_out[layer, rows, :]
            b = 2.0 * b_now[layer, rows, :] - b_old[layer, rows, :] + vertical(ext, layer, rows)
            flat, deep = flat_in[layer, rows, :], deep_in[layer, rows, :]
            one = one_in[layer, rows, :] + a * flat
            two = two_in[layer, rows, :] + (a + b) * deep + b * flat

            @pl.when(core == 0)
            def _():
                keep_out[layer, rows, :] = one
                send_out[layer + 2, rows, :] = two

            @pl.when(core != 0)
            def _():
                send_out[layer, rows, :] = one
                keep_out[layer + 2, rows, :] = two

        return 0

    lax.fori_loop(0, depth, image, 0)
    gain = a_out
    gain[0:2] = lo_next[...] - 2.0 * lo_first[1] + lo_first[0]
    gain[2:4] = hi_next[...] - 2.0 * hi_first[1] + hi_first[0]
    plane = width * length
    here = info[1] - info[0]

    @pl.when((here >= -2 * plane) & (here < 0))
    def _():
        add_at(gain, here + 2 * plane, -pulse[0, 0])

    @pl.when((here >= depth * plane) & (here < (depth + 2) * plane))
    def _():
        add_at(gain, here - (depth - 2) * plane, -pulse[0, 0])

    def w(layer):
        return ext[layer + 2]

    low = (
        lo_share[0] - w(0) * gain[0],
        lo_share[1] + (16.0 * w(0) - w(1)) * gain[1],
    )
    high = (
        hi_share[0] + (16.0 * w(depth - 1) - w(depth - 2)) * gain[2],
        hi_share[1] - w(depth - 1) * gain[3],
    )
    change = [move[n] * (flat_two[l] + deep_two[l]) for n, l in enumerate(ends)]

    def finish(first, second):
        for n in range(2):
            first[depth + n] = low[n]
            second[n] = high[n]
        for n, l in enumerate(ends):
            second[l + 2] = second[l + 2] + change[n]

    @pl.when(core == 0)
    def _():
        finish(keep_out, send_out)

    @pl.when(core != 0)
    def _():
        finish(send_out, keep_out)


def receivers_kernel(info, receivers, count, cells, which):
    size = info[3]
    count[0] = 0

    def look(n, found):
        cell = receivers[0, n] - info[0]
        inside = (cell >= 0) & (cell < size)

        cells[found] = jnp.where(inside, cell, 0)
        which[found] = n
        return found + jnp.where(inside, 1, 0)

    count[0] = lax.fori_loop(0, receivers.shape[1], look, 0, unroll=8)


def quad_kernel(info, own, from_core, from_side, from_both, out):
    core, side = info[2], info[4]
    rows = own.shape[1]
    mine = own[...]
    for c in range(2):
        near = jnp.where(core == c, mine, from_core[...])
        far = jnp.where(core == c, from_side[...], from_both[...])
        out[:, rows * c : rows * (c + 1), :] = jnp.where(side == 0, near, far)
        out[:, rows * (2 + c) : rows * (3 + c), :] = jnp.where(side == 0, far, near)


def model_kernel(pieces, info, count, *refs):
    size = len(pieces)
    own, other = refs[:size], refs[size : 2 * size]
    low, high, stiff, stretch, lo_out, hi_out = refs[2 * size :]
    core, line = info[2], info[5]
    _, width, _ = stiff.shape
    band = own[0].shape[1]
    lines = width // band
    for mine, theirs, (steps, first) in zip(own, other, pieces):
        rows = pl.ds(pl.multiple_of(lax.rem(line + steps, lines) * band, band), band)
        for i in range(mine.shape[0]):
            layer = first + i - 2
            x, y = mine[i], theirs[i]
            vel = jnp.where(core == 0, x, y)
            rest = jnp.where(core == 0, y, x)
            k = vel * vel * (1.0 / 12.0)
            if layer < 0:
                lo_out[layer + 2, rows, :] = k * low[layer + 2, rows, :]
                above = rest * rest * (1.0 / 12.0)
                hi_out[layer + 2, rows, :] = above * high[layer + 2, rows, :]
            else:
                stiff[layer, rows, :] = k
                stretch[layer, rows, :] = 1.0 + 2.0 * rest


def split_kernel(info, keep, got, *outs):
    line = info[5]
    width = keep.shape[1]
    band = outs[0].shape[1]
    lines = width // band
    half = keep.shape[0] // 2
    for i, steps in enumerate((0, 1, 7, 2, 6, 3, 5)):
        rows = pl.ds(pl.multiple_of(lax.rem(line + steps, lines) * band, band), band)
        outs[i][...] = keep[:, rows, :] + got[:, rows, :]
    rows = pl.ds(pl.multiple_of(lax.rem(line + 4, lines) * band, band), band)
    outs[7][...] = keep[:half, rows, :] + got[:half, rows, :]
    outs[8][...] = keep[half:, rows, :] + got[half:, rows, :]


def relay_kernel(plus, minus, from_minus, from_plus, low, high, plus_out, minus_out):
    half = low.shape[0]
    plus_out[...] = plus[...] + from_minus[...]
    minus_out[...] = minus[...] + from_plus[...]
    plus_out[0:half] = plus_out[0:half] + low[...]
    minus_out[half:] = minus_out[half:] + high[...]


def lines_kernel(info, own, r1, r2, r3, r4, keep, send, straight, across):
    core, side = info[2], info[4]
    total = (own[...] + (r1[...] + r2[...])) + (r3[...] + r4[...])
    layers, rows, _ = keep.shape
    near = jnp.where(side == 0, total[:, :rows], total[:, rows:])
    far = jnp.where(side == 0, total[:, rows:], total[:, :rows])
    keep[...] = near
    send[...] = far
    straight[...] = jnp.where(core == 0, near[layers - 2 :], near[:2])
    across[...] = jnp.where(core == 0, far[layers - 2 :], far[:2])


def sides_kernel(info, keep, got, straight, across, mine, send):
    core = info[2]
    layers, width, _ = keep.shape
    rows = width // 2

    def place(first, count, total):
        low, high = total[:, :rows, :], total[:, rows:, :]
        mine[first : first + count] = jnp.where(core == 0, low, high)
        send[first : first + count] = jnp.where(core == 0, high, low)

    place(0, layers, keep[...] + got[...])
    place(layers, 2, straight[...] + across[...])


def gradient_kernel(info, mine, got, vel, eps, vel_out, eps_out):
    core = info[2]
    depth = vel.shape[0]
    one = jnp.where(core == 0, mine[:depth], got[:depth]) * (1.0 / 12.0)
    two = jnp.where(core == 0, got[2 : depth + 2], mine[2 : depth + 2]) * (1.0 / 12.0)
    from_above = jnp.where(core == 0, mine[depth + 2 :], got[depth + 2 :])
    from_below = jnp.where(core == 0, got[depth + 2 :], mine[depth + 2 :])
    v = vel[...]
    stiff = v * v
    vel_out[...] = 2.0 * v * ((1.0 + 2.0 * eps[...]) * one + two)
    for layer in range(2):
        top = depth - 2 + layer
        vel_out[layer] = vel_out[layer] + 2.0 * v[layer] * (from_below[layer] / stiff[layer])
        vel_out[top] = vel_out[top] + 2.0 * v[top] * (from_above[layer] / stiff[top])
    eps_out[...] = 2.0 * stiff * one


def on_device(
    velocity, epsilon, forward_state, adjoint_state, source_cell, wavelet, receiver_cells, residuals
):
    depth, share, length = velocity.shape
    width = forward_state.shape[3]
    shots = lax.axis_size("shot")
    slabs = lax.axis_size("dom")
    lines = shots // 4
    field = shape(depth, width, length)
    ends = shape(2, width, length)
    shot = lax.axis_index("shot")
    core, side, line = shot % 2, (shot // 2) % 2, shot // 4
    info = jnp.stack(
        [
            lax.axis_index("dom") * (depth * width * length),
            source_cell[0],
            core,
            jnp.int32(depth * width * length),
            side,
            line,
        ]
    ).astype(jnp.int32)

    up = [(i, i + 1) for i in range(slabs - 1)]
    down = [(i + 1, i) for i in range(slabs - 1)]

    def halos(lo, hi):
        return lax.ppermute(hi, "dom", up), lax.ppermute(lo, "dom", down)

    def swap(x, mask):
        return lax.ppermute(x, "shot", [(s, s ^ mask) for s in range(shots)])

    def from_line(x, steps):
        pairs = [(s, ((s // 4 - steps) % lines) * 4 + s % 4) for s in range(shots)]
        return lax.ppermute(x, "shot", pairs)

    below, above = halos(velocity[:2], velocity[depth - 2 :])
    first_part = jnp.concatenate([below, velocity], axis=0)
    second_part = jnp.concatenate([above, epsilon], axis=0)
    mine = jnp.where(core == 0, first_part, second_part)
    theirs = jnp.where(core == 0, second_part, first_part)
    from_side = swap(mine, 2)
    from_both = swap(theirs, 3)
    from_core = swap(theirs, 1)
    low_end, high_end = (
        jnp.concatenate(
            [forward_state[0, 2:4, rows], adjoint_state[0, 1:2, rows] + adjoint_state[0, 3:4, rows]], axis=0
        )
        for rows in (slice(0, 2), slice(depth - 2, depth))
    )
    q_lo, q_hi = halos(low_end, high_end)
    quad = call(
        quad_kernel,
        [shape(depth + 2, 4 * share, length)],
        (info, mine, from_core, from_side, from_both),
        1,
    )[0]
    half = depth // 2 + 1
    n2, m2 = from_line(quad, 2), from_line(quad, -2)
    n1, m1 = from_line(quad, 1), from_line(quad, -1)
    n3, m3 = from_line(n2, 1), from_line(m2, -1)
    low, high = from_line(n2[:half], 2), from_line(m2[half:], -2)
    blocks = (quad, n1, m1, n2, m2, n3, m3, low, high)
    pieces = ((0, 0), (1, 0), (7, 0), (2, 0), (6, 0), (3, 0), (5, 0), (4, 0), (4, half))
    other = tuple(swap(x, 1) for x in blocks)
    spots = jax.ShapeDtypeStruct((receiver_cells.shape[1] + 1,), jnp.int32)
    found = call(
        receivers_kernel,
        [jax.ShapeDtypeStruct((1,), jnp.int32), spots, spots],
        (info, receiver_cells),
        2,
        out_specs=[SMEM] * 3,
    )
    stiff, stretch, w_lo, w_hi = call(
        functools.partial(model_kernel, pieces),
        [field, field, ends, ends],
        (info, found[0], *blocks, *other, q_lo[2], q_hi[2]),
        2,
    )
    ext = pltpu.VMEM((depth + 4, width, length), jnp.float32)
    plane = pltpu.VMEM((depth, width, length), jnp.float32)
    model = (stiff, stretch)

    def forward(moment, outs, *args):
        body = functools.partial(forward_kernel, moment)
        return call(body, outs, (info, wavelet, *args), 2, [ext])

    def adjoint(moment, outs, *args):
        body = functools.partial(adjoint_kernel, moment)
        return call(body, outs, (info, *found, residuals, *args), 5, [ext])

    six = [field, field, ends, ends, field, field]
    p2, q2, lo, hi, flat1, deep1 = forward(0, six, forward_state, *model, q_lo, q_hi)
    q2_lo, q2_hi = halos(lo, hi)
    a4, b4, lo, hi = adjoint(3, six[:4], adjoint_state, *model, w_lo, w_hi)
    w3_lo, w3_hi = halos(lo, hi)
    p3, q3, lo, hi, flat2, deep2 = forward(1, six, forward_state, p2, q2, *model, q2_lo, q2_hi)
    q3_lo, q3_hi = halos(lo, hi)
    a3, b3, lo, hi = adjoint(2, six[:4], adjoint_state, a4, b4, *model, w3_lo, w3_hi)
    w2_lo, w2_hi = halos(lo, hi)
    a2, b2, one, two = adjoint(1, [field] * 4, a4, a3, b3, b4, *model, flat2, deep2)
    p4, q4, one, two = forward(2, [field] * 4, p2, p3, q3, q2, *model, q3_lo, q3_hi, a3, b3, one, two)
    one, two, lo_share, hi_share = call(
        last_kernel,
        [field, field, ends, ends],
        (p4, q4, a4, b4, one, two, w3_lo, w3_hi),
        0,
        [ext],
    )
    middle = call(inner_kernel, [shape(depth - 4, width, length)], (a2, b2, a3, *model))[0]
    parts = shape(depth + 2, width, length)
    keep, send = call(
        final_kernel,
        [parts, parts],
        (info, *found, residuals, wavelet, a2, b2, a3, b3, *model, w2_lo, w2_hi)
        + (flat2, deep2, flat1, deep1, one, two, q_lo, q_hi, q2_lo, q2_hi, lo_share, hi_share, middle),
        6,
        [ext, plane, plane, pltpu.VMEM((4, width, length), jnp.float32)],
    )

    band = shape(depth + 2, 4 * share, length)
    half_band = shape(half, 4 * share, length)
    got = swap(send, 1)
    own, s1, t1, s2, t2, s3, t3, low, high = call(
        split_kernel, [band] * 7 + [half_band] * 2, (info, keep, got), 1
    )
    g3, h3 = from_line(s3, -1), from_line(t3, 1)
    g4, h4 = from_line(low, -2), from_line(high, 2)
    s2, t2 = call(relay_kernel, [band] * 2, (s2, t2, g3, h3, g4, h4))
    got = [from_line(s2, -2), from_line(t2, 2), from_line(s1, -1), from_line(t1, 1)]

    def to_slab(x, mask):
        pairs = []
        for s in range(shots):
            for d in range(slabs):
                target = d - 1 if s % 2 == 0 else d + 1
                if 0 <= target < slabs:
                    pairs.append((s * slabs + d, (s ^ mask) * slabs + target))
        return lax.ppermute(x, ("shot", "dom"), pairs)

    pair, rest = shape(depth + 2, 2 * share, length), shape(2, 2 * share, length)
    keep, send, straight, across = call(lines_kernel, [pair, pair, rest, rest], (info, own, *got), 1)
    quarter = shape(depth + 4, share, length)
    keep, send = call(
        sides_kernel,
        [quarter, quarter],
        (info, keep, swap(send, 2), to_slab(straight, 0), to_slab(across, 2)),
        1,
    )
    vel_grad, eps_grad = call(
        gradient_kernel,
        [shape(depth, share, length)] * 2,
        (info, keep, swap(send, 1), velocity, epsilon),
        1,
    )
    return vel_grad, eps_grad


def solution(mesh):
    placed = (
        P("dom", "shot", None),
        P("dom", "shot", None),
        P("shot", None, "dom", None, None),
        P("shot", None, "dom", None, None),
        P("shot"),
        P("shot", None),
        P("shot", None),
        P("shot", None, None),
    )

    return jax.shard_map(
        on_device,
        mesh=mesh,
        in_specs=placed,
        out_specs=(P("dom", "shot", None), P("dom", "shot", None)),
        check_vma=False,
    )
```
